32 devices in a mesh: space: 8 (over z, y), rep: 4 (over x, core).
Axes of the slice: x: 2, y: 2, z: 4, core: 2. Of those that a mesh axis runs over, the one named last changes fastest.
Arguments:
- volumes: bfloat16 [4, 8, 8, 4, 16, 256], P('rep', 'space'), may hold values from -6 to 6
- grad_parts: bfloat16 [4, 2, 6912, 256], P('rep', None, 'space'), may hold values from -6 to 6
- master_weights: float32 [2, 6912, 256], P(None, 'space'), may hold values from -0.078125 to 0.078125
- moment_first: float32 [4, 2, 6912, 256], P('rep', None, 'space'), may hold values from -12 to 12
- moment_second: float32 [4, 2, 6912, 256], P('rep', None, 'space'), may hold values from 1 to 30
- owner: int32 [2, 32], replicated, may hold values from 0 to 3
Outputs:
- features: bfloat16 [4, 8, 8, 4, 16, 256], P('rep', 'space')
- new_weights: float32 [2, 1769472], P(None, ('space', 'rep'))
- moment_first_out: float32 [4, 2, 6912, 256], P('rep', None, 'space')
- moment_second_out: float32 [4, 2, 6912, 256], P('rep', None, 'space')
The draws below stay inside these ranges and needn't reach their ends.
Inputs may be any that keep to these rules, and one draw needn't show every extreme that they name: owner[f, p] is the replica whose state slot holds the optimizer state of panel p of filter f, rows p * 216 to (p + 1) * 216 - 1; replicas may own unequal numbers of panels.
All inputs are finite; a program needn't handle non-finite values.
Results may differ from the reference program's by a relative error of at most 0.0095.
Values may be sent and summed in bfloat16 or wider, within the bound.
No kernel may reach another device: no remote copies, remote signals or barrier semaphores. Data moves between devices by JAX's collectives and lax.ppermute only.
A program may use at most 64 MiB of HBM per device.

```python
import math
import jax
import jax.numpy as jnp
import numpy as np
from jax import lax

C = 256
TAPS = 27
FILTERS = 2
PANELS = 32
GY = 2
GZ = 2
BX = 8
BY = 4
BZ = 16
PANEL_ROWS = 216
BRICKS = 8
VOLUMES = 4
N_SPACE = 8
N_REP = 4


def set_ends(entries, own_key, least, high):
    index_at = [jax.random.randint(jax.random.fold_in(own_key, axis), (), 0, length) for axis, length in enumerate(entries.shape)]
    widest = entries.shape.index(max(entries.shape))
    next_to = index_at[:widest] + [(index_at[widest] + 1) % entries.shape[widest]] + index_at[widest + 1:]
    return entries.at[tuple(index_at)].set(least).at[tuple(next_to)].set(high)


def steps_of(key, extent, pieces, least, largest):
    factor_of, own = 1.0, jax.random.fold_in(key, 6)
    for position, blocks in pieces:
        heights = jnp.exp(jax.random.uniform(jax.random.fold_in(own, position), (blocks,), jnp.float32, least / len(pieces), largest / len(pieces)))
        factor_of = factor_of * jnp.repeat(heights, extent[position] // blocks).reshape([-1 if axis == position else 1 for axis in range(len(extent))])
    return factor_of


def rank_table(number_of, lean):
    weights = [(1 << 20) // math.isqrt(grade ** lean) + 1 for grade in range(1, number_of + 1)]
    spread = 1 + sum(weights) // (1 << 30)
    return np.cumsum(np.array([max(1, weight // spread) for weight in weights]))


def skewed_ids(stream_key, extent, amount, lean):
    grid = rank_table(amount, lean)
    lot = jax.random.randint(jax.random.fold_in(stream_key, 1), extent, 0, int(grid[amount - 1]))
    grade = jnp.searchsorted(jnp.asarray(grid, jnp.int32), lot, side="right")
    return jax.random.permutation(jax.random.fold_in(stream_key, 2), amount)[grade].astype(jnp.int32)


def normal_values(own_key, shape, spread, limit, split=(), kind=jnp.bfloat16):
    gain = steps_of(own_key, shape, split, -0.22, 0.18) if split else 1.0
    values = jax.random.normal(own_key, shape, jnp.float32) * spread * gain
    return jnp.minimum(jnp.maximum(values, -limit), limit).astype(kind)


def setup_inputs(seed: int = 0) -> dict:
    splits = jax.random.split(jax.random.key(seed), 7)
    volumes = normal_values(splits[0], (VOLUMES, BRICKS, BX, BY, BZ, C), 1.0, 6.0, ((0, 4), (1, 8)))
    grad_parts = normal_values(splits[1], (VOLUMES, FILTERS, TAPS * C, C), 1.0, 6.0, ((0, 4), (2, 8)))
    master_weights = normal_values(splits[2], (FILTERS, TAPS * C, C), (TAPS * C) ** -0.5, 0.078125, ((1, 8),), jnp.float32)
    moment_first = normal_values(splits[3], (VOLUMES, FILTERS, TAPS * C, C), 2.0, 12.0, ((0, 4), (2, 8)), jnp.float32)
    moment_second = jnp.clip(jnp.exp(math.log(30.0) - 3.4011974 * jax.random.uniform(splits[4], (VOLUMES, FILTERS, TAPS * C, C), jnp.float32) ** steps_of(splits[4], (VOLUMES, FILTERS, TAPS * C, C), ((0, 4), (2, 8)), -0.2, 0.2)), 1.0, 30.0)
    owner = set_ends(skewed_ids(splits[5], (FILTERS, PANELS), N_REP, 2), jax.random.fold_in(splits[5], 3), 0, N_REP - 1).astype(jnp.int32)
    return {"volumes": volumes, "grad_parts": grad_parts, "master_weights": master_weights, "moment_first": moment_first, "moment_second": moment_second, "owner": owner}


def conv_layer(field, filter_rows):
    extent_x, extent_y, extent_z, channels = field.shape
    padded = jnp.pad(field, ((1, 1), (1, 1), (1, 1), (0, 0))).astype(jnp.float32)
    taps_filter = filter_rows.astype(jnp.float32)
    summed = jnp.zeros((extent_x * extent_y * extent_z, taps_filter.shape[1]), jnp.float32)
    for shift_x in range(3):
        for shift_y in range(3):
            for shift_z in range(3):
                tap_index = (shift_x * 3 + shift_y) * 3 + shift_z
                window = padded[shift_x:shift_x + extent_x, shift_y:shift_y + extent_y, shift_z:shift_z + extent_z]
                weights_tap = taps_filter[tap_index * channels:(tap_index + 1) * channels]
                summed = summed + jnp.dot(window.reshape(-1, channels), weights_tap, preferred_element_type=jnp.float32)
    return summed.reshape(extent_x, extent_y, extent_z, -1)

def reference(volumes, grad_parts, master_weights, moment_first, moment_second, owner):
    summed_grad = lax.optimization_barrier(jnp.sum(grad_parts.astype(jnp.float32), axis=0))
    first_new = 0.9 * moment_first + 0.1 * summed_grad[None]
    second_new = 0.95 * moment_second + 0.05 * (summed_grad * summed_grad)[None]
    owner_rows = jnp.repeat(owner, PANEL_ROWS, axis=1)
    replicas = lax.broadcasted_iota(jnp.int32, (N_REP, 1, 1, 1), 0)
    owned = replicas == owner_rows[None, :, :, None]
    first_out = jnp.where(owned, first_new, moment_first)
    second_out = jnp.where(owned, second_new, moment_second)
    first_own = lax.optimization_barrier(jnp.sum(jnp.where(owned, first_new, 0.0), axis=0))
    second_own = lax.optimization_barrier(jnp.sum(jnp.where(owned, second_new, 0.0), axis=0))
    corr_one = 1.0 - 0.9 ** 10
    corr_two = 1.0 - 0.95 ** 10
    update = first_own / corr_one / (jnp.sqrt(second_own / corr_two) + 1e-08) + 0.1 * master_weights
    new_master = master_weights - 0.004 * update
    new_weights = new_master.reshape(FILTERS, -1)
    filters = new_master.astype(jnp.bfloat16)
    grid_x = N_SPACE // (GY * GZ)
    whole = volumes.reshape(N_REP, grid_x, GY, GZ, BX, BY, BZ, C)
    whole = whole.transpose(0, 1, 4, 2, 5, 3, 6, 7).reshape(N_REP, grid_x * BX, GY * BY, GZ * BZ, C)

    def layers(field):
        hidden = jax.nn.gelu(conv_layer(field, filters[0]), approximate=True).astype(jnp.bfloat16)
        return jax.nn.gelu(conv_layer(hidden, filters[1]), approximate=True).astype(jnp.bfloat16)
    result = lax.map(layers, whole)
    result = result.reshape(N_REP, grid_x, BX, GY, BY, GZ, BZ, C).transpose(0, 1, 3, 5, 2, 4, 6, 7)
    features = result.reshape(N_REP, N_SPACE, BX, BY, BZ, C)
    return (features, new_weights, first_out, second_out)
```

```python
import functools

import jax
import jax.numpy as jnp
from jax import lax
from jax.experimental import pallas as pl
from jax.experimental.pallas import tpu as pltpu
from jax.sharding import PartitionSpec as P

GY = 2
GZ = 2
PANEL_ROWS = 216


def swap(value, axis, stride):
    count = lax.axis_size(axis)
    return lax.ppermute(value, axis, [(source, source ^ stride) for source in range(count)])


def passed_along(value, axis, steps):
    count = lax.axis_size(axis)
    first, last = (max(0, -steps), min(count, count - steps))
    return lax.ppermute(value, axis, [(source, source + steps) for source in range(first, last)])


def pick(flag, one, other):
    return jnp.where(flag, one, other)


def extend_brick(brick, coords, strides, grid):
    current = brick
    for dim in range(3):
        length = current.shape[dim]
        first = lax.slice_in_dim(current, 0, 1, 1, dim)
        last = lax.slice_in_dim(current, length - 1, length, 1, dim)
        if grid[dim] == 2:
            low = coords[dim] == 0
            came = swap(pick(low, last, first), "space", strides[dim])
            none = jnp.zeros_like(came)
            lower, upper = pick(low, none, came), pick(low, came, none)
        else:
            none = jnp.zeros_like(first)
            lower = pick(coords[dim] > 0, passed_along(last, "space", strides[dim]), none)
            upper = pick(
                coords[dim] < grid[dim] - 1, passed_along(first, "space", -strides[dim]), none
            )
        current = jnp.concatenate([lower, current, upper], axis=dim)
    return current


def conv_kernel(places, span, where_ref, field_ref, *refs):
    pieces, (out_ref, weights, lines, sems) = refs[: len(places)], refs[len(places) :]
    space_pos, row_pos, col_pos = where_ref[0], where_ref[1], where_ref[2]
    rows_dev, height = span
    copies = []
    for piece_ref, place in zip(pieces, places):
        for slot, (space_mask, row_mask, col_mask) in enumerate(place):
            start = (space_pos ^ space_mask) * rows_dev + (row_pos ^ row_mask) * height
            target = weights.at[col_pos ^ col_mask, pl.ds(pl.multiple_of(start, 8), height), :]
            copy = pltpu.make_async_copy(piece_ref.at[slot], target, sems.at[len(copies)])
            copy.start()
            copies.append(copy)
    extent_x, extent_y, extent_z, channels = out_ref.shape
    for along_x in range(extent_x + 2):
        field = field_ref[along_x].astype(jnp.float32)
        for shift in range(3):
            lines[along_x, :, :, shift * channels : (shift + 1) * channels] = field[
                :, shift : shift + extent_z
            ].astype(lines.dtype)
    for copy in copies:
        copy.wait()
    depth = 3 * channels
    total = jnp.zeros((extent_x * extent_y * extent_z, channels), jnp.float32)
    for shift_x in range(3):
        for shift_y in range(3):
            start = (shift_x * 3 + shift_y) * depth
            window = lines[shift_x : shift_x + extent_x, shift_y : shift_y + extent_y]
            taps = jnp.concatenate(
                [weights[0, start : start + depth, :], weights[1, start : start + depth, :]], axis=1
            )
            total = total + jnp.dot(
                window.reshape(-1, depth), taps, preferred_element_type=jnp.float32
            )
    out_ref[...] = jax.nn.gelu(total, approximate=True).astype(out_ref.dtype).reshape(out_ref.shape)


def convolve(extended, pieces, places, span, position):
    shape = (extended.shape[0] - 2, extended.shape[1] - 2, extended.shape[2] - 2, extended.shape[3])
    channels = shape[3]
    cells = shape[0] * shape[1] * shape[2]
    rows = 27 * channels
    count = sum(len(place) for place in places)
    return pl.pallas_call(
        functools.partial(conv_kernel, places, span),
        out_shape=jax.ShapeDtypeStruct(shape, jnp.bfloat16),
        in_specs=[
            pl.BlockSpec(memory_space=pltpu.SMEM),
            pl.BlockSpec(memory_space=pltpu.VMEM),
        ]
        + [pl.BlockSpec(memory_space=pl.ANY)] * len(pieces),
        out_specs=pl.BlockSpec(memory_space=pltpu.VMEM),
        scratch_shapes=[
            pltpu.VMEM((2, rows, channels // 2), jnp.bfloat16),
            pltpu.VMEM((shape[0] + 2, shape[1] + 2, shape[2], 3 * channels), jnp.bfloat16),
            pltpu.SemaphoreType.DMA((count,)),
        ],
        compiler_params=pltpu.CompilerParams(vmem_limit_bytes=40 * 2**20),
        cost_estimate=pl.CostEstimate(
            flops=2 * cells * rows * channels,
            bytes_accessed=2 * rows * channels + 4 * cells * channels,
            transcendentals=cells * channels,
        ),
    )(position, extended, *pieces)


def gathered(piece, row_shares):
    strides = []
    stride = lax.axis_size("space") // 2
    while stride:
        strides.append(stride)
        stride //= 2
    held, masks = piece[None], [(0, 0)]
    for stride in strides[:-2]:
        held = jnp.concatenate([held, swap(held, "space", stride)])
        masks = masks + [(space ^ stride, row) for space, row in masks]
    moved_z = [(space ^ strides[-2], row) for space, row in masks]
    beside = swap(held, "space", strides[-2])

    def along_y(places):
        return [(space ^ strides[-1], row) for space, row in places]

    def along_x(places):
        return [(space, row ^ 1) for space, row in places]

    held_y, beside_y = swap(held, "space", strides[-1]), swap(beside, "space", strides[-1])
    found = [(held, masks), (beside, moved_z), (held_y, along_y(masks)), (beside_y, along_y(moved_z))]
    if row_shares == 2:
        held_x, beside_x = swap(held, "rep", 2), swap(beside, "rep", 2)
        found += [
            (held_x, along_x(masks)),
            (beside_x, along_x(moved_z)),
            (swap(held_x, "space", strides[-1]), along_y(along_x(masks))),
            (swap(beside_y, "rep", 2), along_x(along_y(moved_z))),
        ]
    arrays, places = [], []
    for array, place in found:
        arrays += [array, swap(array, "rep", 1)]
        places += [tuple((s, r, c) for s, r in place) for c in range(2)]
    return arrays, tuple(places)


def shards(volumes, grad_parts, master_weights, moment_first, moment_second, owner):
    filter_count, rows_dev, channels = master_weights.shape
    half = channels // 2
    panels_dev = rows_dev // PANEL_ROWS
    replicas = lax.axis_size("rep")
    row_shares = 2 if replicas % 4 == 0 and rows_dev % 16 == 0 else 1
    height = rows_dev // row_shares
    space_pos = lax.axis_index("space")
    rep_pos = lax.axis_index("rep")
    col_pos = rep_pos & 1
    row_pos = (rep_pos >> 1) & (row_shares - 1)
    left, top = col_pos == 0, row_pos == 0
    owner_local = lax.dynamic_slice_in_dim(owner, space_pos * panels_dev, panels_dev, 1)
    owned = (jnp.repeat(owner_local, PANEL_ROWS, axis=1) == rep_pos)[:, :, None]

    grid = (lax.axis_size("space") // (GY * GZ), GY, GZ)
    strides = (GY * GZ, GZ, 1)
    coords = (space_pos // (GY * GZ), space_pos // GZ % GY, space_pos % GZ)
    extended = extend_brick(volumes[0, 0], coords, strides, grid)

    def own_columns(array):
        return pick(left, array[..., :half], array[..., half:])

    def other_columns(array):
        return pick(left, array[..., half:], array[..., :half])

    def own_rows(array):
        if row_shares == 1:
            return array
        return pick(top, array[..., :height, :], array[..., height:, :])

    corr_one = 1.0 - 0.9**10
    corr_two = 1.0 - 0.95**10
    shares, sums, pieces = [], [], []
    for index in range(filter_count):
        kept = jnp.stack(
            [
                grad_parts[0, index].astype(jnp.float32),
                jnp.where(owned[index], moment_first[0, index], 0.0),
                jnp.where(owned[index], moment_second[0, index], 0.0),
            ]
        ).astype(jnp.bfloat16)
        stride = replicas // 2
        while stride >= 2 * row_shares:
            came = swap(kept, "rep", stride).astype(jnp.float32)
            kept = (kept.astype(jnp.float32) + came).astype(jnp.bfloat16)
            stride //= 2
        came = swap(other_columns(kept), "rep", 1)
        state = own_columns(kept).astype(jnp.float32) + came.astype(jnp.float32)
        if row_shares == 2:
            sent = pick(top, state[:, height:], state[:, :height]).astype(jnp.bfloat16)
            came = swap(sent, "rep", 2)
            state = own_rows(state) + came.astype(jnp.float32)
        grad, first, second = state[0], state[1], state[2]
        first = 0.9 * first + 0.1 * grad
        second = 0.95 * second + 0.05 * (grad * grad)
        master = own_rows(own_columns(master_weights[index]))
        update = first / corr_one / (jnp.sqrt(second / corr_two) + 1e-08) + 0.1 * master
        share = master - 0.004 * update
        shares.append(share)
        sums.append(grad.astype(jnp.bfloat16))
        pieces.append(share.astype(jnp.bfloat16))

    position = jnp.stack([space_pos, row_pos, col_pos]).astype(jnp.int32)
    span = (rows_dev, height)

    def rebuilt(share):
        if row_shares == 2:
            came = swap(share, "rep", 2)
            share = pick(
                top, jnp.concatenate([share, came], -2), jnp.concatenate([came, share], -2)
            )
        came = swap(share, "rep", 1)
        return pick(left, jnp.concatenate([share, came], -1), jnp.concatenate([came, share], -1))

    hidden = extended
    for index in range(filter_count):
        if index:
            hidden = extend_brick(hidden, coords, strides, grid)
        arrays, places = gathered(pieces[index], row_shares)
        hidden = convolve(hidden, arrays, places, span, position)

    summed_grad = rebuilt(jnp.stack(sums)).astype(jnp.float32)
    first_new = 0.9 * moment_first[0] + 0.1 * summed_grad
    second_new = 0.95 * moment_second[0] + 0.05 * (summed_grad * summed_grad)
    first_out = jnp.where(owned, first_new, moment_first[0])[None]
    second_out = jnp.where(owned, second_new, moment_second[0])[None]

    share = jnp.stack(shares)
    if replicas == 2 * row_shares:
        middle = height // 2
        sent = pick(left, share[:, middle:], share[:, :middle])
        kept = pick(left, share[:, :middle], share[:, middle:])
        came = swap(sent, "rep", 1)
        new_weights = pick(
            left, jnp.concatenate([kept, came], -1), jnp.concatenate([came, kept], -1)
        ).reshape(filter_count, -1)
    else:
        length = rows_dev * channels // replicas
        new_weights = lax.dynamic_slice_in_dim(
            rebuilt(share).reshape(filter_count, -1), rep_pos * length, length, 1
        )
    return (hidden[None, None], new_weights, first_out, second_out)


def solution(mesh):
    placed = (
        P("rep", "space", None, None, None, None),
        P("rep", None, "space", None),
        P(None, "space", None),
        P("rep", None, "space", None),
        P("rep", None, "space", None),
        P(),
    )
    return jax.shard_map(
        shards,
        mesh=mesh,
        in_specs=placed,
        out_specs=(
            P("rep", "space", None, None, None, None),
            P(None, ("space", "rep")),
            P("rep", None, "space", None),
            P("rep", None, "space", None),
        ),
        check_vma=False,
    )
```

```python
import functools

import jax
import jax.numpy as jnp
from jax import lax
from jax.experimental import pallas as pl
from jax.experimental.pallas import tpu as pltpu
from jax.sharding import PartitionSpec as P

GY = 2
GZ = 2
PANEL_ROWS = 216


def swap(value, axis, stride):
    count = lax.axis_size(axis)
    return lax.ppermute(value, axis, [(source, source ^ stride) for source in range(count)])


def passed_along(value, axis, steps):
    count = lax.axis_size(axis)
    first, last = (max(0, -steps), min(count, count - steps))
    return lax.ppermute(value, axis, [(source, source + steps) for source in range(first, last)])


def pick(flag, one, other):
    return jnp.where(flag, one, other)


def extend_brick(brick, coords, strides, grid):
    current = brick
    for dim in range(3):
        length = current.shape[dim]
        first = lax.slice_in_dim(current, 0, 1, 1, dim)
        last = lax.slice_in_dim(current, length - 1, length, 1, dim)
        if grid[dim] == 2:
            low = coords[dim] == 0
            came = swap(pick(low, last, first), "space", strides[dim])
            none = jnp.zeros_like(came)
            lower, upper = pick(low, none, came), pick(low, came, none)
        else:
            none = jnp.zeros_like(first)
            lower = pick(coords[dim] > 0, passed_along(last, "space", strides[dim]), none)
            upper = pick(
                coords[dim] < grid[dim] - 1, passed_along(first, "space", -strides[dim]), none
            )
        current = jnp.concatenate([lower, current, upper], axis=dim)
    return current


def conv_kernel(places, span, where_ref, field_ref, *refs):
    pieces, (out_ref, weights, lines) = refs[: len(places)], refs[len(places) :]
    space_pos, row_pos, col_pos = where_ref[0], where_ref[1], where_ref[2]
    rows_dev, height = span
    extent_x, extent_y, extent_z, channels = out_ref.shape
    for piece_ref, place in zip(pieces, places):
        for slot, (space_mask, row_mask, col_mask) in enumerate(place):
            start = (space_pos ^ space_mask) * rows_dev + (row_pos ^ row_mask) * height
            weights[col_pos ^ col_mask, pl.ds(pl.multiple_of(start, 8), height), :] = piece_ref[slot]
    for along_x in range(extent_x + 2):
        field = field_ref[along_x].astype(jnp.float32)
        for shift in range(3):
            lines[along_x, :, :, shift * channels : (shift + 1) * channels] = field[
                :, shift : shift + extent_z
            ].astype(lines.dtype)
    depth = 3 * channels
    total = jnp.zeros((extent_x * extent_y * extent_z, channels), jnp.float32)
    for shift_x in range(3):
        for shift_y in range(3):
            start = (shift_x * 3 + shift_y) * depth
            window = lines[shift_x : shift_x + extent_x, shift_y : shift_y + extent_y]
            taps = jnp.concatenate(
                [weights[0, start : start + depth, :], weights[1, start : start + depth, :]], axis=1
            )
            total = total + jnp.dot(
                window.reshape(-1, depth), taps, preferred_element_type=jnp.float32
            )
    out_ref[...] = jax.nn.gelu(total, approximate=True).astype(out_ref.dtype).reshape(out_ref.shape)


def convolve(extended, pieces, places, span, position):
    shape = (extended.shape[0] - 2, extended.shape[1] - 2, extended.shape[2] - 2, extended.shape[3])
    channels = shape[3]
    cells = shape[0] * shape[1] * shape[2]
    rows = 27 * channels
    return pl.pallas_call(
        functools.partial(conv_kernel, places, span),
        out_shape=jax.ShapeDtypeStruct(shape, jnp.bfloat16),
        in_specs=[
            pl.BlockSpec(memory_space=pltpu.SMEM),
            pl.BlockSpec(memory_space=pltpu.VMEM),
        ]
        + [pl.BlockSpec(memory_space=pltpu.VMEM)] * len(pieces),
        out_specs=pl.BlockSpec(memory_space=pltpu.VMEM),
        scratch_shapes=[
            pltpu.VMEM((2, rows, channels // 2), jnp.bfloat16),
            pltpu.VMEM((shape[0] + 2, shape[1] + 2, shape[2], 3 * channels), jnp.bfloat16),
        ],
        compiler_params=pltpu.CompilerParams(vmem_limit_bytes=40 * 2**20),
        cost_estimate=pl.CostEstimate(
            flops=2 * cells * rows * channels,
            bytes_accessed=2 * rows * channels + 4 * cells * channels,
            transcendentals=cells * channels,
        ),
    )(position, extended, *pieces)


def split_kernel(index, where_ref, owner_ref, grad_ref, first_ref, second_ref, kept_ref, sent_ref):
    panel = pl.program_id(0)
    owned = owner_ref[index, where_ref[0] * pl.num_programs(0) + panel] == where_ref[3]
    left = where_ref[2] == 0
    half = kept_ref.shape[-1]
    parts = (
        grad_ref[0, 0].astype(jnp.float32),
        jnp.where(owned, first_ref[0, 0], 0.0),
        jnp.where(owned, second_ref[0, 0], 0.0),
    )
    for slot, part in enumerate(parts):
        one, other = part[:, :half], part[:, half:]
        kept_ref[slot] = jnp.where(left, one, other).astype(kept_ref.dtype)
        sent_ref[slot] = jnp.where(left, other, one).astype(sent_ref.dtype)


def split_state(index, position, owner, grad_parts, moment_first, moment_second):
    rows, channels = grad_parts.shape[2:]
    half = channels // 2
    array = pl.BlockSpec((1, 1, PANEL_ROWS, channels), lambda panel, *_: (0, index, panel, 0))
    part = pl.BlockSpec((3, PANEL_ROWS, half), lambda panel, *_: (0, panel, 0))
    shape = jax.ShapeDtypeStruct((3, rows, half), jnp.bfloat16)
    return pl.pallas_call(
        functools.partial(split_kernel, index),
        out_shape=(shape, shape),
        grid_spec=pltpu.PrefetchScalarGridSpec(
            num_scalar_prefetch=2,
            grid=(rows // PANEL_ROWS,),
            in_specs=[array, array, array],
            out_specs=[part, part],
        ),
        cost_estimate=pl.CostEstimate(
            flops=4 * rows * channels, bytes_accessed=16 * rows * channels, transcendentals=0
        ),
    )(position, owner, grad_parts, moment_first, moment_second)


def across_kernel(where_ref, kept_ref, came_ref, sent_ref):
    height = sent_ref.shape[1]
    rows = pl.ds(pl.multiple_of((1 - where_ref[1]) * height, 8), height)
    for slot in range(3):
        total = kept_ref[slot, rows, :].astype(jnp.float32) + came_ref[slot, rows, :].astype(jnp.float32)
        sent_ref[slot] = total.astype(sent_ref.dtype)


def across(position, kept, came, height):
    vmem = pl.BlockSpec(memory_space=pltpu.VMEM)
    return pl.pallas_call(
        across_kernel,
        out_shape=jax.ShapeDtypeStruct((3, height, kept.shape[2]), jnp.bfloat16),
        in_specs=[pl.BlockSpec(memory_space=pltpu.SMEM), vmem, vmem],
        out_specs=vmem,
        cost_estimate=pl.CostEstimate(
            flops=3 * height * kept.shape[2],
            bytes_accessed=18 * height * kept.shape[2],
            transcendentals=0,
        ),
    )(position, kept, came)


def update_kernel(where_ref, kept_ref, came_ref, master_ref, *refs):
    share_ref, piece_ref, sum_ref = refs[-3:]
    height = share_ref.shape[0]
    rows = pl.ds(pl.multiple_of(where_ref[1] * height, 8), height)
    state = []
    for slot in range(3):
        total = kept_ref[slot, rows, :].astype(jnp.float32) + came_ref[slot, rows, :].astype(jnp.float32)
        for crossed_ref in refs[:-3]:
            total = total + crossed_ref[slot].astype(jnp.float32)
        state.append(total)
    grad, first, second = state
    first = 0.9 * first + 0.1 * grad
    second = 0.95 * second + 0.05 * (grad * grad)
    corr_one = 1.0 - 0.9**10
    corr_two = 1.0 - 0.95**10
    master = master_ref[...]
    update = first / corr_one / (jnp.sqrt(second / corr_two) + 1e-08) + 0.1 * master
    share = master - 0.004 * update
    share_ref[...] = share
    piece_ref[...] = share.astype(piece_ref.dtype)
    sum_ref[...] = grad.astype(sum_ref.dtype)


def updated(position, kept, came, master, crossed):
    vmem = pl.BlockSpec(memory_space=pltpu.VMEM)
    rounded = jax.ShapeDtypeStruct(master.shape, jnp.bfloat16)
    size = master.shape[0] * master.shape[1]
    return pl.pallas_call(
        update_kernel,
        out_shape=(jax.ShapeDtypeStruct(master.shape, jnp.float32), rounded, rounded),
        in_specs=[pl.BlockSpec(memory_space=pltpu.SMEM)] + [vmem] * (3 + len(crossed)),
        out_specs=(vmem, vmem, vmem),
        cost_estimate=pl.CostEstimate(
            flops=20 * size, bytes_accessed=30 * size, transcendentals=2 * size
        ),
    )(position, kept, came, master, *crossed)


def gathered(piece, row_shares, last):
    strides = []
    stride = lax.axis_size("space") // 2
    while stride:
        strides.append(stride)
        stride //= 2
    held, masks = piece[None], [(0, 0)]
    for stride in strides[:-2]:
        held = jnp.concatenate([held, swap(held, "space", stride)])
        masks = masks + [(space ^ stride, row) for space, row in masks]

    def moved(found, *ways):
        array, places = found
        for way in ways:
            if way == "x":
                array = swap(array, "rep", 2)
                places = [(space, row ^ 1) for space, row in places]
            else:
                stride = strides[-1] if way == "y" else strides[-2]
                array = swap(array, "space", stride)
                places = [(space ^ stride, row) for space, row in places]
        return array, places

    own = (held, masks)
    if row_shares == 1:
        z, y = moved(own, "z"), moved(own, "y")
        found = [own, z, y, moved(y, "z")]
    else:
        z, x, y = moved(own, "z"), moved(own, "x"), moved(own, "y")
        xy, yz, zx = moved(x, "y"), moved(y, "z"), moved(z, "x")
        corner = moved({"y": zx, "z": xy, "x": yz}[last], last)
        found = [own, z, x, y, xy, yz, zx, corner]
    arrays, places = [], []
    for array, place in found:
        arrays += [array, swap(array, "rep", 1)]
        places += [tuple((s, r, c) for s, r in place) for c in range(2)]
    return arrays, tuple(places)


def shards(volumes, grad_parts, master_weights, moment_first, moment_second, owner):
    filter_count, rows_dev, channels = master_weights.shape
    half = channels // 2
    panels_dev = rows_dev // PANEL_ROWS
    replicas = lax.axis_size("rep")
    row_shares = 2 if replicas % 4 == 0 and rows_dev % 16 == 0 else 1
    height = rows_dev // row_shares
    space_pos = lax.axis_index("space")
    rep_pos = lax.axis_index("rep")
    col_pos = rep_pos & 1
    row_pos = (rep_pos >> 1) & (row_shares - 1)
    left, top = col_pos == 0, row_pos == 0
    owner_local = lax.dynamic_slice_in_dim(owner, space_pos * panels_dev, panels_dev, 1)
    owned = (jnp.repeat(owner_local, PANEL_ROWS, axis=1) == rep_pos)[:, :, None]
    position = jnp.stack([space_pos, row_pos, col_pos, rep_pos]).astype(jnp.int32)

    grid = (lax.axis_size("space") // (GY * GZ), GY, GZ)
    strides = (GY * GZ, GZ, 1)
    coords = (space_pos // (GY * GZ), space_pos // GZ % GY, space_pos % GZ)

    def own_columns(array):
        return pick(left, array[..., :half], array[..., half:])

    def own_rows(array):
        if row_shares == 1:
            return array
        return pick(top, array[..., :height, :], array[..., height:, :])

    masters = [own_rows(own_columns(master_weights[index])) for index in range(filter_count)]
    split = []
    for index in range(filter_count):
        kept, sent = split_state(index, position, owner, grad_parts, moment_first, moment_second)
        stride = replicas // 2
        while stride >= 2 * row_shares:
            kept, sent = [
                (part.astype(jnp.float32) + swap(part, "rep", stride).astype(jnp.float32)).astype(
                    jnp.bfloat16
                )
                for part in (kept, sent)
            ]
            stride //= 2
        split.append((kept, swap(sent, "rep", 1)))
    crossing = []
    for kept, came in split:
        crossing.append([across(position, kept, came, height)] if row_shares == 2 else [])
    brick = volumes[0, 0]
    if row_shares == 2:
        brick, _ = lax.optimization_barrier((brick, crossing[-1][0]))
    extended = extend_brick(brick, coords, strides, grid)
    shares, sums, pieces = [], [], []
    for (kept, came), master, sends in zip(split, masters, crossing):
        crossed = [swap(sent, "rep", 2) for sent in sends]
        share, piece, summed = updated(position, kept, came, master, crossed)
        shares.append(share)
        pieces.append(piece)
        sums.append(summed)

    span = (rows_dev, height)

    def rebuilt(share):
        if row_shares == 2:
            came = swap(share, "rep", 2)
            share = pick(
                top, jnp.concatenate([share, came], -2), jnp.concatenate([came, share], -2)
            )
        came = swap(share, "rep", 1)
        return pick(left, jnp.concatenate([share, came], -1), jnp.concatenate([came, share], -1))

    hidden = extended
    for index in range(filter_count):
        if index:
            hidden = extend_brick(hidden, coords, strides, grid)
        arrays, places = gathered(pieces[index], row_shares, "yz"[index % 2])
        hidden = convolve(hidden, arrays, places, span, position)

    summed_grad = rebuilt(jnp.stack(sums)).astype(jnp.float32)
    first_new = 0.9 * moment_first[0] + 0.1 * summed_grad
    second_new = 0.95 * moment_second[0] + 0.05 * (summed_grad * summed_grad)
    first_out = jnp.where(owned, first_new, moment_first[0])[None]
    second_out = jnp.where(owned, second_new, moment_second[0])[None]

    share = jnp.stack(shares)
    if replicas == 2 * row_shares:
        middle = height // 2
        sent = pick(left, share[:, middle:], share[:, :middle])
        kept = pick(left, share[:, :middle], share[:, middle:])
        came = swap(sent, "rep", 1)
        new_weights = pick(
            left, jnp.concatenate([kept, came], -1), jnp.concatenate([came, kept], -1)
        ).reshape(filter_count, -1)
    else:
        length = rows_dev * channels // replicas
        new_weights = lax.dynamic_slice_in_dim(
            rebuilt(share).reshape(filter_count, -1), rep_pos * length, length, 1
        )
    return (hidden[None, None], new_weights, first_out, second_out)


def solution(mesh):
    placed = (
        P("rep", "space", None, None, None, None),
        P("rep", None, "space", None),
        P(None, "space", None),
        P("rep", None, "space", None),
        P("rep", None, "space", None),
        P(),
    )
    return jax.shard_map(
        shards,
        mesh=mesh,
        in_specs=placed,
        out_specs=(
            P("rep", "space", None, None, None, None),
            P(None, ("space", "rep")),
            P("rep", None, "space", None),
            P("rep", None, "space", None),
        ),
        check_vma=False,
    )
```

```python
import functools

import jax
import jax.numpy as jnp
from jax import lax
from jax.experimental import pallas as pl
from jax.experimental.pallas import tpu as pltpu
from jax.sharding import PartitionSpec as P


GY = 2
GZ = 2
PANEL_ROWS = 216


def swap(value, axis, stride):
    count = lax.axis_size(axis)
    return lax.ppermute(value, axis, [(source, source ^ stride) for source in range(count)])


def passed_along(value, axis, steps):
    count = lax.axis_size(axis)
    first, last = (max(0, -steps), min(count, count - steps))
    return lax.ppermute(value, axis, [(source, source + steps) for source in range(first, last)])


def pick(flag, one, other):
    return jnp.where(flag, one, other)


def extend_brick(brick, coords, strides, grid):
    current = brick
    for dim in range(3):
        length = current.shape[dim]
        first = lax.slice_in_dim(current, 0, 1, 1, dim)
        last = lax.slice_in_dim(current, length - 1, length, 1, dim)
        if grid[dim] == 2:
            low = coords[dim] == 0
            came = swap(pick(low, last, first), "space", strides[dim])
            none = jnp.zeros_like(came)
            lower, upper = pick(low, none, came), pick(low, came, none)
        else:
            none = jnp.zeros_like(first)
            lower = pick(coords[dim] > 0, passed_along(last, "space", strides[dim]), none)
            upper = pick(
                coords[dim] < grid[dim] - 1, passed_along(first, "space", -strides[dim]), none
            )
        current = jnp.concatenate([lower, current, upper], axis=dim)
    return current


def place_of(row_shares):
    rep_pos = lax.axis_index("rep")
    return lax.axis_index("space"), (rep_pos >> 1) & (row_shares - 1), rep_pos & 1


def conv_kernel(places, span, field_ref, *refs):
    pieces, (out_ref, weights, lines) = refs[: len(places)], refs[len(places) :]
    rows_dev, height = span
    space_pos, row_pos, col_pos = place_of(rows_dev // height)
    extent_x, extent_y, extent_z, channels = out_ref.shape
    for piece_ref, place in zip(pieces, places):
        for slot, (space_mask, row_mask, col_mask) in enumerate(place):
            start = (space_pos ^ space_mask) * rows_dev + (row_pos ^ row_mask) * height
            weights[col_pos ^ col_mask, pl.ds(pl.multiple_of(start, 8), height), :] = piece_ref[slot]
    for along_x in range(extent_x + 2):
        field = field_ref[along_x].astype(jnp.float32)
        for shift in range(3):
            lines[along_x, :, :, shift * channels : (shift + 1) * channels] = field[
                :, shift : shift + extent_z
            ].astype(lines.dtype)
    depth = 3 * channels
    total = jnp.zeros((extent_x * extent_y * extent_z, channels), jnp.float32)
    for shift_x in range(3):
        for shift_y in range(3):
            start = (shift_x * 3 + shift_y) * depth
            window = lines[shift_x : shift_x + extent_x, shift_y : shift_y + extent_y]
            taps = jnp.concatenate(
                [weights[0, start : start + depth, :], weights[1, start : start + depth, :]], axis=1
            )
            total = total + jnp.dot(
                window.reshape(-1, depth), taps, preferred_element_type=jnp.float32
            )
    out_ref[...] = jax.nn.gelu(total, approximate=True).astype(out_ref.dtype).reshape(out_ref.shape)


def convolve(extended, pieces, places, span):
    shape = (extended.shape[0] - 2, extended.shape[1] - 2, extended.shape[2] - 2, extended.shape[3])
    channels = shape[3]
    cells = shape[0] * shape[1] * shape[2]
    rows = 27 * channels
    return pl.pallas_call(
        functools.partial(conv_kernel, places, span),
        out_shape=jax.ShapeDtypeStruct(shape, jnp.bfloat16),
        in_specs=[pl.BlockSpec(memory_space=pltpu.VMEM)] * (1 + len(pieces)),
        out_specs=pl.BlockSpec(memory_space=pltpu.VMEM),
        scratch_shapes=[
            pltpu.VMEM((2, rows, channels // 2), jnp.bfloat16),
            pltpu.VMEM((shape[0] + 2, shape[1] + 2, shape[2], 3 * channels), jnp.bfloat16),
        ],
        compiler_params=pltpu.CompilerParams(vmem_limit_bytes=16 * 2**20),
        cost_estimate=pl.CostEstimate(
            flops=2 * cells * rows * channels,
            bytes_accessed=2 * rows * channels + 4 * cells * channels,
            transcendentals=cells * channels,
        ),
    )(extended, *pieces)


def split_kernel(index, *refs):
    arrays, all_owners, (kept_ref, sent_ref) = refs[:3], refs[3], refs[-8:-6]
    buffers, owners, sems, owner_sem = refs[-6:-3], refs[-3], refs[-2], refs[-1]
    panels = buffers[0].shape[0]
    space_pos, rep_pos = lax.axis_index("space"), lax.axis_index("rep")
    left = rep_pos & 1 == 0
    half = kept_ref.shape[2]
    copy_owners = pltpu.make_async_copy(all_owners, owners, owner_sem)
    copy_owners.start()
    copies = []
    for panel in range(panels):
        rows = pl.ds(panel * PANEL_ROWS, PANEL_ROWS)
        for slot in range(3):
            copies.append(
                pltpu.make_async_copy(
                    arrays[slot].at[0, index, rows, :],
                    buffers[slot].at[panel],
                    sems.at[panel, slot],
                )
            )
            copies[-1].start()
    copy_owners.wait()
    for panel in range(panels):
        owned = owners[index, space_pos * panels + panel] == rep_pos
        rows = slice(panel * PANEL_ROWS, (panel + 1) * PANEL_ROWS)
        for slot in range(3):
            copies[3 * panel + slot].wait()
            part = buffers[slot][panel].astype(jnp.float32)
            if slot:
                part = jnp.where(owned, part, 0.0)
            one, other = part[:, :half], part[:, half:]
            kept_ref[slot, rows, :] = jnp.where(left, one, other).astype(kept_ref.dtype)
            sent_ref[slot, rows, :] = jnp.where(left, other, one).astype(sent_ref.dtype)


def split_state(index, owner, *arrays, after=()):
    rows, channels = arrays[0].shape[2:]
    half = channels // 2
    panels = rows // PANEL_ROWS
    shape = jax.ShapeDtypeStruct((3, rows, half), jnp.bfloat16)
    vmem = pl.BlockSpec(memory_space=pltpu.VMEM)
    held = [pltpu.with_memory_space_constraint(array, pltpu.HBM) for array in (*arrays, owner)]
    return pl.pallas_call(
        functools.partial(split_kernel, index),
        out_shape=(shape, shape),
        in_specs=[pl.BlockSpec(memory_space=pltpu.HBM)] * len(held)
        + [pl.BlockSpec(memory_space=pl.ANY)] * len(after),
        out_specs=(vmem, vmem),
        scratch_shapes=[
            pltpu.VMEM((panels, PANEL_ROWS, channels), array.dtype) for array in arrays
        ]
        + [
            pltpu.SMEM(owner.shape, owner.dtype),
            pltpu.SemaphoreType.DMA((panels, 3)),
            pltpu.SemaphoreType.DMA,
        ],
        compiler_params=pltpu.CompilerParams(vmem_limit_bytes=6 * 2**20),
        cost_estimate=pl.CostEstimate(
            flops=4 * rows * channels, bytes_accessed=16 * rows * channels, transcendentals=0
        ),
    )(*held, *after)


def across_kernel(kept_ref, came_ref, sent_ref):
    height = sent_ref.shape[1]
    row_pos = place_of(2)[1]
    rows = pl.ds(pl.multiple_of((1 - row_pos) * height, 8), height)
    for slot in range(3):
        total = kept_ref[slot, rows, :].astype(jnp.float32) + came_ref[slot, rows, :].astype(jnp.float32)
        sent_ref[slot] = total.astype(sent_ref.dtype)


def across(kept, came, height):
    vmem = pl.BlockSpec(memory_space=pltpu.VMEM)
    return pl.pallas_call(
        across_kernel,
        out_shape=jax.ShapeDtypeStruct((3, height, kept.shape[2]), jnp.bfloat16),
        in_specs=[vmem, vmem],
        out_specs=vmem,
        compiler_params=pltpu.CompilerParams(vmem_limit_bytes=4 * 2**20),
        cost_estimate=pl.CostEstimate(
            flops=3 * height * kept.shape[2],
            bytes_accessed=18 * height * kept.shape[2],
            transcendentals=0,
        ),
    )(kept, came)


def update_kernel(index, all_master, kept_ref, came_ref, *refs):
    piece_ref, sum_ref, master_ref, sem = refs[-4:]
    height, half = piece_ref.shape
    _, row_pos, col_pos = place_of(kept_ref.shape[1] // height)
    rows = pl.ds(pl.multiple_of(row_pos * height, 8), height)
    columns = pl.ds(pl.multiple_of(col_pos * half, 128), half)
    copy = pltpu.make_async_copy(all_master.at[index, rows, columns], master_ref, sem)
    copy.start()
    state = []
    for slot in range(3):
        total = kept_ref[slot, rows, :].astype(jnp.float32) + came_ref[slot, rows, :].astype(jnp.float32)
        for crossed_ref in refs[:-4]:
            total = total + crossed_ref[slot].astype(jnp.float32)
        state.append(total)
    grad, first, second = state
    first = 0.9 * first + 0.1 * grad
    second = 0.95 * second + 0.05 * (grad * grad)
    corr_one = 1.0 - 0.9**10
    corr_two = 1.0 - 0.95**10
    sum_ref[...] = grad.astype(sum_ref.dtype)
    ratio = first / corr_one / (jnp.sqrt(second / corr_two) + 1e-08)
    copy.wait()
    master = master_ref[...]
    piece_ref[...] = (master - 0.004 * (ratio + 0.1 * master)).astype(piece_ref.dtype)


def updated(index, height, master, kept, came, crossed):
    vmem = pl.BlockSpec(memory_space=pltpu.VMEM)
    half = kept.shape[2]
    rounded = jax.ShapeDtypeStruct((height, half), jnp.bfloat16)
    size = height * half
    return pl.pallas_call(
        functools.partial(update_kernel, index),
        out_shape=(rounded, rounded),
        in_specs=[pl.BlockSpec(memory_space=pltpu.HBM)] + [vmem] * (2 + len(crossed)),
        out_specs=(vmem, vmem),
        scratch_shapes=[pltpu.VMEM((height, half), jnp.float32), pltpu.SemaphoreType.DMA],
        compiler_params=pltpu.CompilerParams(vmem_limit_bytes=4 * 2**20),
        cost_estimate=pl.CostEstimate(
            flops=20 * size, bytes_accessed=30 * size, transcendentals=2 * size
        ),
    )(pltpu.with_memory_space_constraint(master, pltpu.HBM), kept, came, *crossed)


def gathered(piece, row_shares, last):
    strides = []
    stride = lax.axis_size("space") // 2
    while stride:
        strides.append(stride)
        stride //= 2
    held, masks = piece[None], [(0, 0)]
    for stride in strides[:-2]:
        held = jnp.concatenate([held, swap(held, "space", stride)])
        masks = masks + [(space ^ stride, row) for space, row in masks]

    def moved(found, way):
        array, places = found
        if way == "x":
            array = swap(array, "rep", 2)
            places = [(space, row ^ 1) for space, row in places]
        else:
            stride = strides[-1] if way == "y" else strides[-2]
            array = swap(array, "space", stride)
            places = [(space ^ stride, row) for space, row in places]
        return array, places

    own = (held, masks)
    z, y = moved(own, "z"), moved(own, "y")
    yz = moved(y, "z")
    found = [own, z, y, yz]
    if row_shares == 2:
        x = moved(own, "x")
        xy, zx = moved(x, "y"), moved(z, "x")
        corner = moved({"y": zx, "z": xy, "x": yz}[last], last)
        found += [x, xy, zx, corner]
    arrays, places = [], []
    for array, place in found:
        arrays += [array, swap(array, "rep", 1)]
        places += [tuple((s, r, c) for s, r in place) for c in range(2)]
    return arrays, tuple(places)


def shards(volumes, grad_parts, master_weights, moment_first, moment_second, owner):
    filter_count, rows_dev, channels = master_weights.shape
    panels_dev = rows_dev // PANEL_ROWS
    replicas = lax.axis_size("rep")
    row_shares = 2 if replicas % 4 == 0 and rows_dev % 16 == 0 else 1
    height = rows_dev // row_shares
    space_pos = lax.axis_index("space")
    rep_pos = lax.axis_index("rep")
    col_pos = rep_pos & 1
    row_pos = (rep_pos >> 1) & (row_shares - 1)
    left, top = col_pos == 0, row_pos == 0
    owner_local = lax.dynamic_slice_in_dim(owner, space_pos * panels_dev, panels_dev, 1)
    owned = (jnp.repeat(owner_local, PANEL_ROWS, axis=1) == rep_pos)[:, :, None]

    grid = (lax.axis_size("space") // (GY * GZ), GY, GZ)
    strides = (GY * GZ, GZ, 1)
    coords = (space_pos // (GY * GZ), space_pos // GZ % GY, space_pos % GZ)

    split = []
    for index in range(filter_count):
        kept, sent = split_state(
            index,
            owner,
            grad_parts,
            moment_first,
            moment_second,
            after=[split[-1][0]] if split else [],
        )
        stride = replicas // 2
        while stride >= 2 * row_shares:
            kept, sent = [
                (part.astype(jnp.float32) + swap(part, "rep", stride).astype(jnp.float32)).astype(
                    jnp.bfloat16
                )
                for part in (kept, sent)
            ]
            stride //= 2
        split.append((kept, swap(sent, "rep", 1)))
    extended = extend_brick(volumes[0, 0], coords, strides, grid)
    sums, pieces = [], []
    for index, (kept, came) in enumerate(split):
        crossed = []
        if row_shares == 2:
            crossed.append(swap(across(kept, came, height), "rep", 2))
        piece, summed = updated(index, height, master_weights, kept, came, crossed)
        pieces.append(piece)
        sums.append(summed)

    span = (rows_dev, height)

    def rebuilt(share):
        if row_shares == 2:
            came = swap(share, "rep", 2)
            share = pick(
                top, jnp.concatenate([share, came], -2), jnp.concatenate([came, share], -2)
            )
        came = swap(share, "rep", 1)
        return pick(left, jnp.concatenate([share, came], -1), jnp.concatenate([came, share], -1))

    hidden, beside = extended, []
    for index in range(filter_count):
        if index:
            hidden = extend_brick(hidden, coords, strides, grid)
        arrays, places = gathered(pieces[index], row_shares, "yz"[index % 2])
        beside.append(arrays[1][0])
        hidden = convolve(hidden, arrays, places, span)

    summed_grad = rebuilt(jnp.stack(sums)).astype(jnp.float32)
    first_new = 0.9 * moment_first[0] + 0.1 * summed_grad
    second_new = 0.95 * moment_second[0] + 0.05 * (summed_grad * summed_grad)
    first_out = jnp.where(owned, first_new, moment_first[0])[None]
    second_out = jnp.where(owned, second_new, moment_second[0])[None]

    if replicas == 2 * row_shares:
        middle = height // 2

        def own_half(array):
            return pick(left, array[:, :middle], array[:, middle:])

        kept, came = own_half(jnp.stack(pieces)), own_half(jnp.stack(beside))
        new_weights = pick(
            left, jnp.concatenate([kept, came], -1), jnp.concatenate([came, kept], -1)
        ).reshape(filter_count, -1)
    else:
        length = rows_dev * channels // replicas
        new_weights = lax.dynamic_slice_in_dim(
            rebuilt(jnp.stack(pieces)).reshape(filter_count, -1),
            rep_pos * length,
            length,
            1,
        )
    new_weights = new_weights.astype(jnp.float32)
    return (hidden[None, None], new_weights, first_out, second_out)


def solution(mesh):
    placed = (
        P("rep", "space", None, None, None, None),
        P("rep", None, "space", None),
        P(None, "space", None),
        P("rep", None, "space", None),
        P("rep", None, "space", None),
        P(),
    )
    return jax.shard_map(
        shards,
        mesh=mesh,
        in_specs=placed,
        out_specs=(
            P("rep", "space", None, None, None, None),
            P(None, ("space", "rep")),
            P("rep", None, "space", None),
            P("rep", None, "space", None),
        ),
        check_vma=False,
    )
```

```python
import functools

import jax
import jax.numpy as jnp
from jax import lax
from jax.experimental import pallas as pl
from jax.experimental.pallas import tpu as pltpu
from jax.sharding import PartitionSpec as P


GY = 2
GZ = 2
PANEL_ROWS = 216


def swap(value, axis, stride):
    count = lax.axis_size(axis)
    return lax.ppermute(value, axis, [(source, source ^ stride) for source in range(count)])


def passed_along(value, axis, steps):
    count = lax.axis_size(axis)
    first, last = (max(0, -steps), min(count, count - steps))
    return lax.ppermute(value, axis, [(source, source + steps) for source in range(first, last)])


def pick(flag, one, other):
    return jnp.where(flag, one, other)


def extend_brick(brick, coords, strides, grid):
    current = brick
    for dim in range(3):
        length = current.shape[dim]
        first = lax.slice_in_dim(current, 0, 1, 1, dim)
        last = lax.slice_in_dim(current, length - 1, length, 1, dim)
        if grid[dim] == 2:
            low = coords[dim] == 0
            came = swap(pick(low, last, first), "space", strides[dim])
            none = jnp.zeros_like(came)
            lower, upper = pick(low, none, came), pick(low, came, none)
        else:
            none = jnp.zeros_like(first)
            lower = pick(coords[dim] > 0, passed_along(last, "space", strides[dim]), none)
            upper = pick(
                coords[dim] < grid[dim] - 1, passed_along(first, "space", -strides[dim]), none
            )
        current = jnp.concatenate([lower, current, upper], axis=dim)
    return current


def place_of(row_shares):
    rep_pos = lax.axis_index("rep")
    return lax.axis_index("space"), (rep_pos >> 1) & (row_shares - 1), rep_pos & 1


def conv_kernel(places, span, field_ref, *refs):
    pieces, (out_ref, weights, lines) = refs[: len(places)], refs[len(places) :]
    rows_dev, height = span
    space_pos, row_pos, col_pos = place_of(rows_dev // height)
    extent_x, extent_y, extent_z, channels = out_ref.shape
    for piece_ref, place in zip(pieces, places):
        for slot, (space_mask, row_mask, col_mask) in enumerate(place):
            start = (space_pos ^ space_mask) * rows_dev + (row_pos ^ row_mask) * height
            weights[col_pos ^ col_mask, pl.ds(pl.multiple_of(start, 8), height), :] = piece_ref[slot]
    for along_x in range(extent_x + 2):
        field = field_ref[along_x].astype(jnp.float32)
        for shift in range(3):
            lines[along_x, :, :, shift * channels : (shift + 1) * channels] = field[
                :, shift : shift + extent_z
            ].astype(lines.dtype)
    depth = 3 * channels
    total = jnp.zeros((extent_x * extent_y * extent_z, channels), jnp.float32)
    for shift_x in range(3):
        for shift_y in range(3):
            start = (shift_x * 3 + shift_y) * depth
            window = lines[shift_x : shift_x + extent_x, shift_y : shift_y + extent_y]
            taps = jnp.concatenate(
                [weights[0, start : start + depth, :], weights[1, start : start + depth, :]], axis=1
            )
            total = total + jnp.dot(
                window.reshape(-1, depth), taps, preferred_element_type=jnp.float32
            )
    out_ref[...] = jax.nn.gelu(total, approximate=True).astype(out_ref.dtype).reshape(out_ref.shape)


def convolve(extended, pieces, places, span):
    shape = (extended.shape[0] - 2, extended.shape[1] - 2, extended.shape[2] - 2, extended.shape[3])
    channels = shape[3]
    cells = shape[0] * shape[1] * shape[2]
    rows = 27 * channels
    return pl.pallas_call(
        functools.partial(conv_kernel, places, span),
        out_shape=jax.ShapeDtypeStruct(shape, jnp.bfloat16),
        in_specs=[pl.BlockSpec(memory_space=pltpu.VMEM)] * (1 + len(pieces)),
        out_specs=pl.BlockSpec(memory_space=pltpu.VMEM),
        scratch_shapes=[
            pltpu.VMEM((2, rows, channels // 2), jnp.bfloat16),
            pltpu.VMEM((shape[0] + 2, shape[1] + 2, shape[2], 3 * channels), jnp.bfloat16),
        ],
        compiler_params=pltpu.CompilerParams(vmem_limit_bytes=16 * 2**20),
        cost_estimate=pl.CostEstimate(
            flops=2 * cells * rows * channels,
            bytes_accessed=2 * rows * channels + 4 * cells * channels,
            transcendentals=cells * channels,
        ),
    )(extended, *pieces)


def split_kernel(index, *refs):
    arrays, all_owners, (kept_ref, sent_ref) = refs[:3], refs[3], refs[-8:-6]
    buffers, owners, sems, owner_sem = refs[-6:-3], refs[-3], refs[-2], refs[-1]
    panels = buffers[0].shape[0]
    space_pos, rep_pos = lax.axis_index("space"), lax.axis_index("rep")
    left = rep_pos & 1 == 0
    half = kept_ref.shape[2]
    copy_owners = pltpu.make_async_copy(all_owners, owners, owner_sem)
    copy_owners.start()
    copies = []
    for panel in range(panels):
        rows = pl.ds(panel * PANEL_ROWS, PANEL_ROWS)
        for slot in range(3):
            copies.append(
                pltpu.make_async_copy(
                    arrays[slot].at[0, index, rows, :],
                    buffers[slot].at[panel],
                    sems.at[panel, slot],
                )
            )
            copies[-1].start()
    copy_owners.wait()
    for panel in range(panels):
        owned = owners[index, space_pos * panels + panel] == rep_pos
        rows = slice(panel * PANEL_ROWS, (panel + 1) * PANEL_ROWS)
        for slot in range(3):
            copies[3 * panel + slot].wait()
            part = buffers[slot][panel].astype(jnp.float32)
            if slot:
                part = jnp.where(owned, part, 0.0)
            one, other = part[:, :half], part[:, half:]
            kept_ref[slot, rows, :] = jnp.where(left, one, other).astype(kept_ref.dtype)
            sent_ref[slot, rows, :] = jnp.where(left, other, one).astype(sent_ref.dtype)


def split_state(index, owner, *arrays, after=()):
    rows, channels = arrays[0].shape[2:]
    half = channels // 2
    panels = rows // PANEL_ROWS
    shape = jax.ShapeDtypeStruct((3, rows, half), jnp.bfloat16)
    vmem = pl.BlockSpec(memory_space=pltpu.VMEM)
    held = [pltpu.with_memory_space_constraint(array, pltpu.HBM) for array in (*arrays, owner)]
    return pl.pallas_call(
        functools.partial(split_kernel, index),
        out_shape=(shape, shape),
        in_specs=[pl.BlockSpec(memory_space=pltpu.HBM)] * len(held)
        + [pl.BlockSpec(memory_space=pl.ANY)] * len(after),
        out_specs=(vmem, vmem),
        scratch_shapes=[
            pltpu.VMEM((panels, PANEL_ROWS, channels), array.dtype) for array in arrays
        ]
        + [
            pltpu.SMEM(owner.shape, owner.dtype),
            pltpu.SemaphoreType.DMA((panels, 3)),
            pltpu.SemaphoreType.DMA,
        ],
        compiler_params=pltpu.CompilerParams(vmem_limit_bytes=6 * 2**20),
        cost_estimate=pl.CostEstimate(
            flops=4 * rows * channels, bytes_accessed=16 * rows * channels, transcendentals=0
        ),
    )(*held, *after)


def across_kernel(kept_ref, came_ref, sent_ref):
    height = sent_ref.shape[1]
    row_pos = place_of(2)[1]
    rows = pl.ds(pl.multiple_of((1 - row_pos) * height, 8), height)
    for slot in range(3):
        total = kept_ref[slot, rows, :].astype(jnp.float32) + came_ref[slot, rows, :].astype(jnp.float32)
        sent_ref[slot] = total.astype(sent_ref.dtype)


def across(kept, came, height):
    vmem = pl.BlockSpec(memory_space=pltpu.VMEM)
    return pl.pallas_call(
        across_kernel,
        out_shape=jax.ShapeDtypeStruct((3, height, kept.shape[2]), jnp.bfloat16),
        in_specs=[vmem, vmem],
        out_specs=vmem,
        compiler_params=pltpu.CompilerParams(vmem_limit_bytes=4 * 2**20),
        cost_estimate=pl.CostEstimate(
            flops=3 * height * kept.shape[2],
            bytes_accessed=18 * height * kept.shape[2],
            transcendentals=0,
        ),
    )(kept, came)


def fetch_kernel(all_master, *refs):
    master_ref, sem = refs[-2:]
    _, height, half = master_ref.shape
    _, row_pos, col_pos = place_of(all_master.shape[1] // height)
    rows = pl.ds(pl.multiple_of(row_pos * height, 8), height)
    columns = pl.ds(pl.multiple_of(col_pos * half, 128), half)
    copy = pltpu.make_async_copy(all_master.at[:, rows, columns], master_ref, sem)
    copy.start()
    copy.wait()


def fetched(height, half, master, after):
    shape = (master.shape[0], height, half)
    return pl.pallas_call(
        fetch_kernel,
        out_shape=jax.ShapeDtypeStruct(shape, master.dtype),
        in_specs=[pl.BlockSpec(memory_space=pltpu.HBM)]
        + [pl.BlockSpec(memory_space=pl.ANY)] * len(after),
        out_specs=pl.BlockSpec(memory_space=pltpu.VMEM),
        scratch_shapes=[pltpu.SemaphoreType.DMA],
        compiler_params=pltpu.CompilerParams(vmem_limit_bytes=2 * 2**20),
        cost_estimate=pl.CostEstimate(
            flops=0, bytes_accessed=8 * master.shape[0] * height * half, transcendentals=0
        ),
    )(pltpu.with_memory_space_constraint(master, pltpu.HBM), *after)


def update_kernel(index, master_ref, kept_ref, came_ref, *refs):
    piece_ref, sum_ref = refs[-2:]
    height = piece_ref.shape[0]
    row_pos = place_of(kept_ref.shape[1] // height)[1]
    rows = pl.ds(pl.multiple_of(row_pos * height, 8), height)
    state = []
    for slot in range(3):
        total = kept_ref[slot, rows, :].astype(jnp.float32) + came_ref[slot, rows, :].astype(jnp.float32)
        for crossed_ref in refs[:-2]:
            total = total + crossed_ref[slot].astype(jnp.float32)
        state.append(total)
    grad, first, second = state
    first = 0.9 * first + 0.1 * grad
    second = 0.95 * second + 0.05 * (grad * grad)
    corr_one = 1.0 - 0.9**10
    corr_two = 1.0 - 0.95**10
    sum_ref[...] = grad.astype(sum_ref.dtype)
    master = master_ref[index]
    update = first / corr_one / (jnp.sqrt(second / corr_two) + 1e-08) + 0.1 * master
    piece_ref[...] = (master - 0.004 * update).astype(piece_ref.dtype)


def updated(index, master, kept, came, crossed):
    vmem = pl.BlockSpec(memory_space=pltpu.VMEM)
    _, height, half = master.shape
    rounded = jax.ShapeDtypeStruct((height, half), jnp.bfloat16)
    size = height * half
    return pl.pallas_call(
        functools.partial(update_kernel, index),
        out_shape=(rounded, rounded),
        in_specs=[vmem] * (3 + len(crossed)),
        out_specs=(vmem, vmem),
        compiler_params=pltpu.CompilerParams(vmem_limit_bytes=4 * 2**20),
        cost_estimate=pl.CostEstimate(
            flops=20 * size, bytes_accessed=30 * size, transcendentals=2 * size
        ),
    )(master, kept, came, *crossed)


def gathered(piece, row_shares, last):
    strides = []
    stride = lax.axis_size("space") // 2
    while stride:
        strides.append(stride)
        stride //= 2
    held, masks = piece[None], [(0, 0)]
    for stride in strides[:-2]:
        held = jnp.concatenate([held, swap(held, "space", stride)])
        masks = masks + [(space ^ stride, row) for space, row in masks]

    def moved(found, way):
        array, places = found
        if way == "x":
            array = swap(array, "rep", 2)
            places = [(space, row ^ 1) for space, row in places]
        else:
            stride = strides[-1] if way == "y" else strides[-2]
            array = swap(array, "space", stride)
            places = [(space ^ stride, row) for space, row in places]
        return array, places

    own = (held, masks)
    z, y = moved(own, "z"), moved(own, "y")
    yz = moved(y, "z")
    found = [own, z, y, yz]
    if row_shares == 2:
        x = moved(own, "x")
        xy, zx = moved(x, "y"), moved(z, "x")
        corner = moved({"y": zx, "z": xy, "x": yz}[last], last)
        found += [x, xy, zx, corner]
    arrays, places = [], []
    for array, place in found:
        arrays += [array, swap(array, "rep", 1)]
        places += [tuple((s, r, c) for s, r in place) for c in range(2)]
    return arrays, tuple(places)


def shards(volumes, grad_parts, master_weights, moment_first, moment_second, owner):
    filter_count, rows_dev, channels = master_weights.shape
    half = channels // 2
    panels_dev = rows_dev // PANEL_ROWS
    replicas = lax.axis_size("rep")
    row_shares = 2 if replicas % 4 == 0 and rows_dev % 16 == 0 else 1
    height = rows_dev // row_shares
    space_pos = lax.axis_index("space")
    rep_pos = lax.axis_index("rep")
    col_pos = rep_pos & 1
    row_pos = (rep_pos >> 1) & (row_shares - 1)
    left, top = col_pos == 0, row_pos == 0
    owner_local = lax.dynamic_slice_in_dim(owner, space_pos * panels_dev, panels_dev, 1)
    owned = (jnp.repeat(owner_local, PANEL_ROWS, axis=1) == rep_pos)[:, :, None]

    grid = (lax.axis_size("space") // (GY * GZ), GY, GZ)
    strides = (GY * GZ, GZ, 1)
    coords = (space_pos // (GY * GZ), space_pos // GZ % GY, space_pos % GZ)

    split, crossing, after = [], [], []
    for index in range(filter_count):
        kept, sent = split_state(index, owner, grad_parts, moment_first, moment_second, after=after)
        stride = replicas // 2
        while stride >= 2 * row_shares:
            kept, sent = [
                (part.astype(jnp.float32) + swap(part, "rep", stride).astype(jnp.float32)).astype(
                    jnp.bfloat16
                )
                for part in (kept, sent)
            ]
            stride //= 2
        came = swap(sent, "rep", 1)
        split.append((kept, came))
        crossing.append([across(kept, came, height)] if row_shares == 2 else [])
        after = crossing[-1] or [kept]
    master = fetched(height, half, master_weights, after=[split[-1][0]])
    extended = extend_brick(volumes[0, 0], coords, strides, grid)
    sums, pieces = [], []
    for index, (kept, came) in enumerate(split):
        crossed = [swap(sent, "rep", 2) for sent in crossing[index]]
        piece, summed = updated(index, master, kept, came, crossed)
        pieces.append(piece)
        sums.append(summed)

    span = (rows_dev, height)

    def rebuilt(share):
        if row_shares == 2:
            came = swap(share, "rep", 2)
            share = pick(
                top, jnp.concatenate([share, came], -2), jnp.concatenate([came, share], -2)
            )
        came = swap(share, "rep", 1)
        return pick(left, jnp.concatenate([share, came], -1), jnp.concatenate([came, share], -1))

    hidden, beside = extended, []
    for index in range(filter_count):
        if index:
            hidden = extend_brick(hidden, coords, strides, grid)
        arrays, places = gathered(pieces[index], row_shares, "yx"[index % 2])
        beside.append(arrays[1][0])
        hidden = convolve(hidden, arrays, places, span)

    summed_grad = rebuilt(jnp.stack(sums)).astype(jnp.float32)
    first_new = 0.9 * moment_first[0] + 0.1 * summed_grad
    second_new = 0.95 * moment_second[0] + 0.05 * (summed_grad * summed_grad)
    first_out = jnp.where(owned, first_new, moment_first[0])[None]
    second_out = jnp.where(owned, second_new, moment_second[0])[None]

    if replicas == 2 * row_shares:
        middle = height // 2

        def own_half(array):
            return pick(left, array[:, :middle], array[:, middle:])

        kept, came = own_half(jnp.stack(pieces)), own_half(jnp.stack(beside))
        new_weights = pick(
            left, jnp.concatenate([kept, came], -1), jnp.concatenate([came, kept], -1)
        ).reshape(filter_count, -1)
    else:
        length = rows_dev * channels // replicas
        new_weights = lax.dynamic_slice_in_dim(
            rebuilt(jnp.stack(pieces)).reshape(filter_count, -1),
            rep_pos * length,
            length,
            1,
        )
    new_weights = new_weights.astype(jnp.float32)
    return (hidden[None, None], new_weights, first_out, second_out)


def solution(mesh):
    placed = (
        P("rep", "space", None, None, None, None),
        P("rep", None, "space", None),
        P(None, "space", None),
        P("rep", None, "space", None),
        P("rep", None, "space", None),
        P(),
    )
    return jax.shard_map(
        shards,
        mesh=mesh,
        in_specs=placed,
        out_specs=(
            P("rep", "space", None, None, None, None),
            P(None, ("space", "rep")),
            P("rep", None, "space", None),
            P("rep", None, "space", None),
        ),
        check_vma=False,
    )
```

```python
import functools

import jax
import jax.numpy as jnp
from jax import lax
from jax.experimental import pallas as pl
from jax.experimental.pallas import tpu as pltpu
from jax.sharding import PartitionSpec as P


GY = 2
GZ = 2
PANEL_ROWS = 216


def swap(value, axis, stride):
    count = lax.axis_size(axis)
    return lax.ppermute(value, axis, [(source, source ^ stride) for source in range(count)])


def passed_along(value, axis, steps):
    count = lax.axis_size(axis)
    first, last = (max(0, -steps), min(count, count - steps))
    return lax.ppermute(value, axis, [(source, source + steps) for source in range(first, last)])


def pick(flag, one, other):
    return jnp.where(flag, one, other)


def extend_brick(brick, coords, strides, grid):
    current = brick
    for dim in range(3):
        length = current.shape[dim]
        first = lax.slice_in_dim(current, 0, 1, 1, dim)
        last = lax.slice_in_dim(current, length - 1, length, 1, dim)
        if grid[dim] == 2:
            low = coords[dim] == 0
            came = swap(pick(low, last, first), "space", strides[dim])
            none = jnp.zeros_like(came)
            lower, upper = pick(low, none, came), pick(low, came, none)
        else:
            none = jnp.zeros_like(first)
            lower = pick(coords[dim] > 0, passed_along(last, "space", strides[dim]), none)
            upper = pick(
                coords[dim] < grid[dim] - 1, passed_along(first, "space", -strides[dim]), none
            )
        current = jnp.concatenate([lower, current, upper], axis=dim)
    return current


def place_of(row_shares):
    rep_pos = lax.axis_index("rep")
    return lax.axis_index("space"), (rep_pos >> 1) & (row_shares - 1), rep_pos & 1


def conv_kernel(places, span, field_ref, *refs):
    pieces, (out_ref, weights, lines) = refs[: len(places)], refs[len(places) :]
    rows_dev, height = span
    space_pos, row_pos, col_pos = place_of(rows_dev // height)
    extent_x, extent_y, extent_z, channels = out_ref.shape
    for piece_ref, place in zip(pieces, places):
        for slot, (space_mask, row_mask, col_mask) in enumerate(place):
            start = (space_pos ^ space_mask) * rows_dev + (row_pos ^ row_mask) * height
            weights[col_pos ^ col_mask, pl.ds(pl.multiple_of(start, 8), height), :] = piece_ref[slot]
    for along_x in range(extent_x + 2):
        field = field_ref[along_x].astype(jnp.float32)
        for shift in range(3):
            lines[along_x, :, :, shift * channels : (shift + 1) * channels] = field[
                :, shift : shift + extent_z
            ].astype(lines.dtype)
    depth = 3 * channels
    total = jnp.zeros((extent_x * extent_y * extent_z, channels), jnp.float32)
    for shift_x in range(3):
        for shift_y in range(3):
            start = (shift_x * 3 + shift_y) * depth
            window = lines[shift_x : shift_x + extent_x, shift_y : shift_y + extent_y]
            taps = jnp.concatenate(
                [weights[0, start : start + depth, :], weights[1, start : start + depth, :]], axis=1
            )
            total = total + jnp.dot(
                window.reshape(-1, depth), taps, preferred_element_type=jnp.float32
            )
    out_ref[...] = jax.nn.gelu(total, approximate=True).astype(out_ref.dtype).reshape(out_ref.shape)


def convolve(extended, pieces, places, span):
    shape = (extended.shape[0] - 2, extended.shape[1] - 2, extended.shape[2] - 2, extended.shape[3])
    channels = shape[3]
    cells = shape[0] * shape[1] * shape[2]
    rows = 27 * channels
    return pl.pallas_call(
        functools.partial(conv_kernel, places, span),
        out_shape=jax.ShapeDtypeStruct(shape, jnp.bfloat16),
        in_specs=[pl.BlockSpec(memory_space=pltpu.VMEM)] * (1 + len(pieces)),
        out_specs=pl.BlockSpec(memory_space=pltpu.VMEM),
        scratch_shapes=[
            pltpu.VMEM((2, rows, channels // 2), jnp.bfloat16),
            pltpu.VMEM((shape[0] + 2, shape[1] + 2, shape[2], 3 * channels), jnp.bfloat16),
        ],
        compiler_params=pltpu.CompilerParams(vmem_limit_bytes=16 * 2**20),
        cost_estimate=pl.CostEstimate(
            flops=2 * cells * rows * channels,
            bytes_accessed=2 * rows * channels + 4 * cells * channels,
            transcendentals=cells * channels,
        ),
    )(extended, *pieces)


def split_kernel(index, *refs):
    arrays, all_owners, (kept_ref, sent_ref) = refs[:3], refs[3], refs[-8:-6]
    buffers, owners, sems, owner_sem = refs[-6:-3], refs[-3], refs[-2], refs[-1]
    panels = buffers[0].shape[0]
    space_pos, rep_pos = lax.axis_index("space"), lax.axis_index("rep")
    left = rep_pos & 1 == 0
    half = kept_ref.shape[2]
    copy_owners = pltpu.make_async_copy(all_owners, owners, owner_sem)
    copy_owners.start()
    copies = []
    for panel in range(panels):
        rows = pl.ds(panel * PANEL_ROWS, PANEL_ROWS)
        for slot in range(3):
            copies.append(
                pltpu.make_async_copy(
                    arrays[slot].at[0, index, rows, :],
                    buffers[slot].at[panel],
                    sems.at[panel, slot],
                )
            )
            copies[-1].start()
    copy_owners.wait()
    for panel in range(panels):
        owned = owners[index, space_pos * panels + panel] == rep_pos
        rows = slice(panel * PANEL_ROWS, (panel + 1) * PANEL_ROWS)
        for slot in range(3):
            copies[3 * panel + slot].wait()
            part = buffers[slot][panel].astype(jnp.float32)
            if slot:
                part = jnp.where(owned, part, 0.0)
            one, other = part[:, :half], part[:, half:]
            kept_ref[slot, rows, :] = jnp.where(left, one, other).astype(kept_ref.dtype)
            sent_ref[slot, rows, :] = jnp.where(left, other, one).astype(sent_ref.dtype)


def split_state(index, owner, *arrays, after=()):
    rows, channels = arrays[0].shape[2:]
    half = channels // 2
    panels = rows // PANEL_ROWS
    shape = jax.ShapeDtypeStruct((3, rows, half), jnp.bfloat16)
    vmem = pl.BlockSpec(memory_space=pltpu.VMEM)
    held = [pltpu.with_memory_space_constraint(array, pltpu.HBM) for array in (*arrays, owner)]
    return pl.pallas_call(
        functools.partial(split_kernel, index),
        out_shape=(shape, shape),
        in_specs=[pl.BlockSpec(memory_space=pltpu.HBM)] * len(held)
        + [pl.BlockSpec(memory_space=pl.ANY)] * len(after),
        out_specs=(vmem, vmem),
        scratch_shapes=[
            pltpu.VMEM((panels, PANEL_ROWS, channels), array.dtype) for array in arrays
        ]
        + [
            pltpu.SMEM(owner.shape, owner.dtype),
            pltpu.SemaphoreType.DMA((panels, 3)),
            pltpu.SemaphoreType.DMA,
        ],
        compiler_params=pltpu.CompilerParams(vmem_limit_bytes=6 * 2**20),
        cost_estimate=pl.CostEstimate(
            flops=4 * rows * channels, bytes_accessed=16 * rows * channels, transcendentals=0
        ),
    )(*held, *after)


def across_kernel(kept_ref, came_ref, sent_ref):
    height = sent_ref.shape[1]
    row_pos = place_of(2)[1]
    rows = pl.ds(pl.multiple_of((1 - row_pos) * height, 8), height)
    for slot in range(3):
        total = kept_ref[slot, rows, :].astype(jnp.float32) + came_ref[slot, rows, :].astype(jnp.float32)
        sent_ref[slot] = total.astype(sent_ref.dtype)


def across(kept, came, height):
    vmem = pl.BlockSpec(memory_space=pltpu.VMEM)
    return pl.pallas_call(
        across_kernel,
        out_shape=jax.ShapeDtypeStruct((3, height, kept.shape[2]), jnp.bfloat16),
        in_specs=[vmem, vmem],
        out_specs=vmem,
        compiler_params=pltpu.CompilerParams(vmem_limit_bytes=4 * 2**20),
        cost_estimate=pl.CostEstimate(
            flops=3 * height * kept.shape[2],
            bytes_accessed=18 * height * kept.shape[2],
            transcendentals=0,
        ),
    )(kept, came)


def fetch_kernel(all_master, *refs):
    master_ref, sem = refs[-2:]
    _, height, half = master_ref.shape
    _, row_pos, col_pos = place_of(all_master.shape[1] // height)
    rows = pl.ds(pl.multiple_of(row_pos * height, 8), height)
    columns = pl.ds(pl.multiple_of(col_pos * half, 128), half)
    copy = pltpu.make_async_copy(all_master.at[:, rows, columns], master_ref, sem)
    copy.start()
    copy.wait()


def fetched(height, half, master, after):
    shape = (master.shape[0], height, half)
    return pl.pallas_call(
        fetch_kernel,
        out_shape=jax.ShapeDtypeStruct(shape, master.dtype),
        in_specs=[pl.BlockSpec(memory_space=pltpu.HBM)]
        + [pl.BlockSpec(memory_space=pl.ANY)] * len(after),
        out_specs=pl.BlockSpec(memory_space=pltpu.VMEM),
        scratch_shapes=[pltpu.SemaphoreType.DMA],
        compiler_params=pltpu.CompilerParams(vmem_limit_bytes=2 * 2**20),
        cost_estimate=pl.CostEstimate(
            flops=0, bytes_accessed=8 * master.shape[0] * height * half, transcendentals=0
        ),
    )(pltpu.with_memory_space_constraint(master, pltpu.HBM), *after)


def update_kernel(index, master_ref, kept_ref, came_ref, *refs):
    piece_ref, sum_ref = refs[-2:]
    height = piece_ref.shape[0]
    row_pos = place_of(kept_ref.shape[1] // height)[1]
    rows = pl.ds(pl.multiple_of(row_pos * height, 8), height)
    state = []
    for slot in range(3):
        total = kept_ref[slot, rows, :].astype(jnp.float32) + came_ref[slot, rows, :].astype(jnp.float32)
        for crossed_ref in refs[:-2]:
            total = total + crossed_ref[slot].astype(jnp.float32)
        state.append(total)
    grad, first, second = state
    first = 0.9 * first + 0.1 * grad
    second = 0.95 * second + 0.05 * (grad * grad)
    corr_one = 1.0 - 0.9**10
    corr_two = 1.0 - 0.95**10
    sum_ref[...] = grad.astype(sum_ref.dtype)
    master = master_ref[index]
    update = first / corr_one / (jnp.sqrt(second / corr_two) + 1e-08) + 0.1 * master
    piece_ref[...] = (master - 0.004 * update).astype(piece_ref.dtype)


def updated(index, master, kept, came, crossed):
    vmem = pl.BlockSpec(memory_space=pltpu.VMEM)
    _, height, half = master.shape
    rounded = jax.ShapeDtypeStruct((height, half), jnp.bfloat16)
    size = height * half
    return pl.pallas_call(
        functools.partial(update_kernel, index),
        out_shape=(rounded, rounded),
        in_specs=[vmem] * (3 + len(crossed)),
        out_specs=(vmem, vmem),
        compiler_params=pltpu.CompilerParams(vmem_limit_bytes=4 * 2**20),
        cost_estimate=pl.CostEstimate(
            flops=20 * size, bytes_accessed=30 * size, transcendentals=2 * size
        ),
    )(master, kept, came, *crossed)


def gathered(piece, row_shares, last, late):
    strides = []
    stride = lax.axis_size("space") // 2
    while stride:
        strides.append(stride)
        stride //= 2
    held, masks = piece[None], [(0, 0)]
    for stride in strides[:-2]:
        held = jnp.concatenate([held, swap(held, "space", stride)])
        masks = masks + [(space ^ stride, row) for space, row in masks]

    def moved(found, way):
        array, places = found
        if way == "x":
            array = swap(array, "rep", 2)
            places = [(space, row ^ 1) for space, row in places]
        else:
            stride = strides[-1] if way == "y" else strides[-2]
            array = swap(array, "space", stride)
            places = [(space ^ stride, row) for space, row in places]
        return array, places

    own = (held, masks)
    z, y = moved(own, "z"), moved(own, "y")
    yz = moved(z, "y") if late else moved(y, "z")
    found = [own, z, y, yz]
    if row_shares == 2:
        x = moved(own, "x")
        xy = moved(y, "x") if late else moved(x, "y")
        zx = moved(z, "x")
        corner = moved({"y": zx, "z": xy, "x": yz}[last], last)
        found += [x, xy, zx, corner]
    arrays, places = [], []
    for array, place in found:
        arrays += [array, swap(array, "rep", 1)]
        places += [tuple((s, r, c) for s, r in place) for c in range(2)]
    return arrays, tuple(places)


def shards(volumes, grad_parts, master_weights, moment_first, moment_second, owner):
    filter_count, rows_dev, channels = master_weights.shape
    half = channels // 2
    panels_dev = rows_dev // PANEL_ROWS
    replicas = lax.axis_size("rep")
    row_shares = 2 if replicas % 4 == 0 and rows_dev % 16 == 0 else 1
    height = rows_dev // row_shares
    space_pos = lax.axis_index("space")
    rep_pos = lax.axis_index("rep")
    col_pos = rep_pos & 1
    row_pos = (rep_pos >> 1) & (row_shares - 1)
    left, top = col_pos == 0, row_pos == 0
    owner_local = lax.dynamic_slice_in_dim(owner, space_pos * panels_dev, panels_dev, 1)
    owned = (jnp.repeat(owner_local, PANEL_ROWS, axis=1) == rep_pos)[:, :, None]

    grid = (lax.axis_size("space") // (GY * GZ), GY, GZ)
    strides = (GY * GZ, GZ, 1)
    coords = (space_pos // (GY * GZ), space_pos // GZ % GY, space_pos % GZ)

    split, crossing, after = [], [], []
    for index in range(filter_count):
        kept, sent = split_state(index, owner, grad_parts, moment_first, moment_second, after=after)
        stride = replicas // 2
        while stride >= 2 * row_shares:
            kept, sent = [
                (part.astype(jnp.float32) + swap(part, "rep", stride).astype(jnp.float32)).astype(
                    jnp.bfloat16
                )
                for part in (kept, sent)
            ]
            stride //= 2
        came = swap(sent, "rep", 1)
        split.append((kept, came))
        crossing.append([across(kept, came, height)] if row_shares == 2 else [])
        after = crossing[-1] or [kept]
    master = fetched(height, half, master_weights, after=[split[-1][0]])
    extended = extend_brick(volumes[0, 0], coords, strides, grid)
    sums, pieces = [], []
    for index, (kept, came) in enumerate(split):
        crossed = [swap(sent, "rep", 2) for sent in crossing[index]]
        piece, summed = updated(index, master, kept, came, crossed)
        pieces.append(piece)
        sums.append(summed)

    span = (rows_dev, height)

    def rebuilt(share):
        if row_shares == 2:
            came = swap(share, "rep", 2)
            share = pick(
                top, jnp.concatenate([share, came], -2), jnp.concatenate([came, share], -2)
            )
        came = swap(share, "rep", 1)
        return pick(left, jnp.concatenate([share, came], -1), jnp.concatenate([came, share], -1))

    hidden, beside = extended, []
    for index in range(filter_count):
        if index:
            hidden = extend_brick(hidden, coords, strides, grid)
        arrays, places = gathered(pieces[index], row_shares, "y", index > 0)
        beside.append(arrays[1][0])
        hidden = convolve(hidden, arrays, places, span)

    summed_grad = rebuilt(jnp.stack(sums)).astype(jnp.float32)
    first_new = 0.9 * moment_first[0] + 0.1 * summed_grad
    second_new = 0.95 * moment_second[0] + 0.05 * (summed_grad * summed_grad)
    first_out = jnp.where(owned, first_new, moment_first[0])[None]
    second_out = jnp.where(owned, second_new, moment_second[0])[None]

    if replicas == 2 * row_shares:
        middle = height // 2

        def own_half(array):
            return pick(left, array[:, :middle], array[:, middle:])

        kept, came = own_half(jnp.stack(pieces)), own_half(jnp.stack(beside))
        new_weights = pick(
            left, jnp.concatenate([kept, came], -1), jnp.concatenate([came, kept], -1)
        ).reshape(filter_count, -1)
    else:
        length = rows_dev * channels // replicas
        new_weights = lax.dynamic_slice_in_dim(
            rebuilt(jnp.stack(pieces)).reshape(filter_count, -1),
            rep_pos * length,
            length,
            1,
        )
    new_weights = new_weights.astype(jnp.float32)
    return (hidden[None, None], new_weights, first_out, second_out)


def solution(mesh):
    placed = (
        P("rep", "space", None, None, None, None),
        P("rep", None, "space", None),
        P(None, "space", None),
        P("rep", None, "space", None),
        P("rep", None, "space", None),
        P(),
    )
    return jax.shard_map(
        shards,
        mesh=mesh,
        in_specs=placed,
        out_specs=(
            P("rep", "space", None, None, None, None),
            P(None, ("space", "rep")),
            P("rep", None, "space", None),
            P("rep", None, "space", None),
        ),
        check_vma=False,
    )
```
